32 devices in a mesh: dp: 16 (over z, y, x), fsdp: 2 (over core).
Axes of the slice: x: 2, y: 2, z: 4, core: 2. Of those that a mesh axis runs over, the one named last changes fastest.
Arguments:
- tokens: bfloat16 [2, 4096, 1024], P(None, ('dp', 'fsdp')), may hold values from -6 to 6
- cotangent: bfloat16 [2, 4096, 1024], P(None, ('dp', 'fsdp')), may hold values from -6 to 6
- seq_offsets: int32 [2, 16, 1], P(None, 'dp'), may hold values from 0 to 15, as said below
- seq_lengths: int32 [2, 16, 1], P(None, 'dp'), may hold values from 178 to 256, as said below
- norm_gain: bfloat16 [1024], P(('dp', 'fsdp')), may hold values from 0.099609375 to 1.8984375
- in_weight: bfloat16 [1024, 4384], P(('dp', 'fsdp')), may hold values from -0.1875 to 0.1875
- conv_weight: bfloat16 [2304, 4], P(('dp', 'fsdp')), may hold values from -3 to 3
- conv_bias: bfloat16 [2304], P(('dp', 'fsdp')), may hold values from -3 to 3
- gate_gain: bfloat16 [2048], P(('dp', 'fsdp')), may hold values from 0.099609375 to 1.8984375
- out_weight: bfloat16 [1024, 2048], P(('dp', 'fsdp')), may hold values from -0.125 to 0.125
- step_bias: float32 [32], replicated, may hold values from -5.3 to -2.3
- decay_log: float32 [32], replicated, may hold values from 0 to 2.77
- skip_scale: float32 [32], replicated, may hold values from 0.5 to 2
Outputs:
- output: bfloat16 [2, 4096, 1024], P(None, ('dp', 'fsdp'))
- input_grad: float32 [2, 4096, 1024], P(None, ('dp', 'fsdp'))
- grad_norm_gain: float32 [1024], P(('dp', 'fsdp'))
- grad_in_weight: float32 [1024, 4384], P(('dp', 'fsdp'))
- grad_conv_weight: float32 [2304, 4], P(('dp', 'fsdp'))
- grad_conv_bias: float32 [2304], P(('dp', 'fsdp'))
- grad_gate_gain: float32 [2048], P(('dp', 'fsdp'))
- grad_out_weight: float32 [1024, 2048], P(('dp', 'fsdp'))
- grad_step_bias: float32 [32], replicated
- grad_decay_log: float32 [32], replicated
- grad_skip_scale: float32 [32], replicated
The draws below stay inside these ranges and needn't reach their ends.
Inputs may be any that keep to these rules, and one draw needn't show every extreme that they name: `seq_offsets`: each stream of 256 positions holds one sequence; positions before and after it are padding. `seq_lengths`: lengths of the sequences whose offsets are given in seq_offsets; every sequence runs past stream position 128.
All inputs are finite; a program needn't handle non-finite values.
Results may differ from the reference program's by a relative error of at most 0.0082.
Values may be sent and summed in bfloat16 or wider, within the bound.
No kernel may reach another device: no remote copies, remote signals or barrier semaphores. Data moves between devices by JAX's collectives and lax.ppermute only.
A program may use at most 192 MiB of HBM per device.

```python
from functools import partial
import jax
import jax.numpy as jnp
from jax import lax

D = 1024
HEADS = 32
HEAD_DIM = 64
STATE = 128
CONV = 4
MB = 2
SEQS = 1
TOK_MB = 128
INNER = 2048
XBC = 2304
PROJ = 4384
TOKENS_MB = 4096
N_DP = 16
N_FSDP = 2


def packing(key):
    base_key = jax.random.fold_in(key, 7)
    key_list = jax.random.split(base_key, 2)
    grid_shape = (MB, N_DP)
    lead_span = max(TOK_MB // 8, 2)
    leading = jax.random.randint(key_list[0], grid_shape, 0, lead_span)
    trailing = jax.random.randint(key_list[1], grid_shape, 0, TOK_MB // 2)
    leading = leading.at[0, 0].set(0).at[0, 1].set(lead_span - 1)
    trailing = trailing.at[0, 0].set(0).at[0, 1].set(TOK_MB // 2 - 1)
    seq_len = N_FSDP * TOK_MB - leading - trailing
    offsets = leading[:, :, None].astype(jnp.int32)
    lengths = seq_len[:, :, None].astype(jnp.int32)
    return (offsets, lengths)


def draw_seq_offsets(key, part):
    return packing(key)[0]


def draw_seq_lengths(key, part):
    return packing(key)[1]


def block_levels(key, shape, cuts, low, top_value):
    def one(dim, blocks):
        heights = jax.random.uniform(jax.random.fold_in(jax.random.fold_in(key, 6), dim), (blocks,), jnp.float32, low / len(cuts), top_value / len(cuts))
        return jnp.repeat(jnp.exp(heights), shape[dim] // blocks).reshape((-1,) + (1,) * (len(shape) - dim - 1))

    level = one(*cuts[0])
    for cut in cuts[1:]:
        level = level * one(*cut)
    return level


def normal_values(rng, dims, scale, bound, shards=(), held_as=jnp.bfloat16):
    values = jax.random.normal(rng, dims, jnp.float32) * scale
    if len(shards) > 0:
        values = block_levels(rng, dims, shards, -0.22, 0.18) * values
    return jnp.clip(values, min=-bound, max=bound).astype(held_as)


def setup_inputs(seed: int = 0) -> dict:
    seeds = jax.random.split(jax.random.key(seed), 14)
    return {
        "tokens": normal_values(seeds[0], (MB, TOKENS_MB, D), 1.0, 6.0, ((1, 32),)),
        "cotangent": normal_values(seeds[1], (MB, TOKENS_MB, D), 1.0, 6.0, ((1, 32),)),
        "seq_offsets": draw_seq_offsets(jax.random.fold_in(seeds[13], 71), 0),
        "seq_lengths": draw_seq_lengths(jax.random.fold_in(seeds[13], 71), 0),
        "norm_gain": jnp.clip(1.0 + 0.18 * jax.random.normal(seeds[4], (D,), jnp.float32), 0.099609375, 1.8984375).astype(jnp.bfloat16),
        "in_weight": normal_values(seeds[5], (D, PROJ), D ** -0.5, 0.1875, ((0, 32),)),
        "conv_weight": normal_values(seeds[6], (XBC, CONV), CONV ** -0.5, 3.0, ((0, 32),)),
        "conv_bias": normal_values(seeds[7], (XBC,), 0.5, 3.0, ((0, 32),)),
        "gate_gain": jnp.clip(1.0 + 0.18 * jax.random.normal(seeds[8], (INNER,), jnp.float32), 0.099609375, 1.8984375).astype(jnp.bfloat16),
        "out_weight": normal_values(seeds[9], (D, INNER), INNER ** -0.5, 0.125, ((0, 32),)),
        "step_bias": jnp.clip(jax.random.uniform(seeds[10], (HEADS,), jnp.float32, -5.3, -2.3), -5.3, -2.3),
        "decay_log": jnp.clip(jax.random.uniform(seeds[11], (HEADS,), jnp.float32, 0.0, 2.77), 0.0, 2.77),
        "skip_scale": jnp.clip(jax.random.uniform(seeds[12], (HEADS,), jnp.float32, 0.5, 2.0), 0.5, 2.0),
    }


EPS = 1e-05
HIGH = lax.Precision.HIGHEST

def segment_of(offsets, lengths, places):
    inside = (places[:, None] >= offsets[None, :]) & (places[:, None] < offsets[None, :] + lengths[None, :])
    labels = jnp.arange(1, offsets.shape[0] + 1, dtype=jnp.int32)
    return (lax.optimization_barrier(jnp.sum(jnp.where(inside, labels[None, :], 0), axis=1)) - 1).astype(jnp.int32)

def prenorm(values, gain):
    return values * lax.rsqrt(lax.optimization_barrier(jnp.mean(values * values, axis=-1, keepdims=True)) + EPS) * gain[None, :]

def gate_norm(pre_out, head_values, skip_scale, gate_in, gate_gain):
    row_count = pre_out.shape[0]
    mixed = (pre_out + skip_scale[None, :, None] * head_values).reshape(row_count, INNER) * jax.nn.silu(gate_in)
    return mixed * lax.rsqrt(lax.optimization_barrier(jnp.mean(mixed * mixed, axis=-1, keepdims=True)) + EPS) * gate_gain[None, :]

def mixer(projected, conv_weight, conv_bias, step_bias, decay_log, skip_scale, gate_gain, segments):
    row_count = projected.shape[0]
    gate_in = projected[:, :INNER]
    xbc_pre = projected[:, INNER:INNER + XBC]
    dt_raw = projected[:, INNER + XBC:]
    convolved = jnp.broadcast_to(conv_bias[None, :], xbc_pre.shape)
    for lag_index in range(CONV):
        moved = jnp.pad(xbc_pre, ((lag_index, 0), (0, 0)))[:row_count]
        moved_segs = jnp.pad(segments, (lag_index, 0), constant_values=-1)[:row_count]
        keep = ((moved_segs == segments) & (segments >= 0)).astype(jnp.float32)
        convolved = convolved + keep[:, None] * moved * conv_weight[None, :, CONV - 1 - lag_index]
    activated = jax.nn.silu(convolved)
    head_values = activated[:, :INNER].reshape(row_count, HEADS, HEAD_DIM)
    write_map = activated[:, INNER:INNER + STATE]
    read_map = activated[:, INNER + STATE:]
    steps = jax.nn.softplus(dt_raw + step_bias[None, :])
    log_decay = -steps * jnp.exp(decay_log)[None, :]
    cumul = jnp.cumsum(log_decay, axis=0)
    order = jnp.arange(row_count, dtype=jnp.int32)
    same_seq = (segments[:, None] == segments[None, :]) & (segments[:, None] >= 0) & (order[:, None] >= order[None, :])
    gram = jnp.dot(read_map, write_map.T, precision=HIGH)
    spread = cumul.T[:, :, None] - cumul.T[:, None, :]
    weights = jnp.exp(jnp.where(same_seq[None], spread, -jnp.inf)) * gram[None] * steps.T[:, None, :]
    pre_out = jnp.einsum('hts,shp->thp', weights, head_values, precision=HIGH)
    return gate_norm(pre_out, head_values, skip_scale, gate_in, gate_gain)

def reference(tokens, cotangent, seq_offsets, seq_lengths, norm_gain, in_weight, conv_weight, conv_bias, gate_gain, out_weight, step_bias, decay_log, skip_scale):
    stream = N_FSDP * TOK_MB
    groups = MB * N_DP
    token_rows = tokens.reshape(groups, stream, D)
    cot_rows = cotangent.reshape(groups, stream, D)
    offset_rows = seq_offsets.reshape(groups, SEQS)
    length_rows = seq_lengths.reshape(groups, SEQS)
    gain_full = norm_gain.astype(jnp.float32)
    conv_full = conv_weight.astype(jnp.float32)
    bias_full = conv_bias.astype(jnp.float32)
    gate_full = gate_gain.astype(jnp.float32)
    dims_rows = (((0,), (0,)), ((), ()))
    dims_cols = (((1,), (1,)), ((), ()))

    def one_stream(sums, inputs):
        source_b, cot_b, offsets, lengths_now = inputs
        places = jnp.arange(stream, dtype=jnp.int32)
        segments = segment_of(offsets, lengths_now, places)
        valid = segments >= 0
        source = source_b.astype(jnp.float32)
        normed, norm_back = jax.vjp(prenorm, source, gain_full)
        normed_b = normed.astype(jnp.bfloat16)
        projected = jnp.dot(normed_b, in_weight, preferred_element_type=jnp.float32)
        gated, mix_back = jax.vjp(partial(mixer, segments=segments), projected, conv_full, bias_full, step_bias, decay_log, skip_scale, gate_full)
        gated_b = gated.astype(jnp.bfloat16)
        branch = lax.dot_general(gated_b, out_weight, dims_cols, preferred_element_type=jnp.float32)
        output_rows = (source + jnp.where(valid[:, None], branch, 0.0)).astype(jnp.bfloat16)
        masked = jnp.where(valid[:, None], cot_b, jnp.zeros((), jnp.bfloat16))
        part_out = lax.dot_general(masked, gated_b, dims_rows, preferred_element_type=jnp.float32)
        d_gated = jnp.dot(masked, out_weight, preferred_element_type=jnp.float32)
        d_projected, part_conv, part_bias, d_step, d_decay, d_skip, part_gate = mix_back(d_gated)
        d_proj_b = d_projected.astype(jnp.bfloat16)
        part_in = lax.dot_general(normed_b, d_proj_b, dims_rows, preferred_element_type=jnp.float32)
        d_normed = lax.dot_general(d_proj_b, in_weight, dims_cols, preferred_element_type=jnp.float32)
        d_source, part_gain = norm_back(d_normed)
        grad_rows = cot_b.astype(jnp.float32) + d_source
        parts = (part_gain, part_in, part_conv, part_bias, part_gate, part_out, d_step, d_decay, d_skip)
        sums = tuple((old + new for old, new in zip(sums, parts)))
        return (sums, (output_rows, grad_rows))
    start = (jnp.zeros((D,), jnp.float32), jnp.zeros((D, PROJ), jnp.float32), jnp.zeros((XBC, CONV), jnp.float32), jnp.zeros((XBC,), jnp.float32), jnp.zeros((INNER,), jnp.float32), jnp.zeros((D, INNER), jnp.float32), jnp.zeros((HEADS,), jnp.float32), jnp.zeros((HEADS,), jnp.float32), jnp.zeros((HEADS,), jnp.float32))
    sums, stacked = lax.scan(one_stream, start, (token_rows, cot_rows, offset_rows, length_rows))
    output = stacked[0].reshape(MB, N_DP * stream, D)
    input_grad = stacked[1].reshape(MB, N_DP * stream, D)
    return (output, input_grad, sums[0], sums[1], sums[2], sums[3], sums[4], sums[5], sums[6], sums[7], sums[8])
```

```python
from functools import partial

import jax
import jax.numpy as jnp
import numpy as np
from jax import lax
from jax.experimental import pallas as pl
from jax.experimental.pallas import tpu as pltpu
from jax.sharding import PartitionSpec as P

HEADS = 32
HEAD_DIM = 64
STATE = 128
CONV = 4
INNER = 2048
XBC = 2304
TAIL = 2432
LANES = 128
BLOCKS = INNER // LANES
EPS = 1e-05
HIGH = lax.Precision.HIGHEST
F32 = jnp.float32
BF16 = jnp.bfloat16
NN = (((1,), (0,)), ((), ()))
NT = (((1,), (1,)), ((), ()))
TN = (((0,), (0,)), ((), ()))


def split(a):
    high = a.astype(BF16)
    return high, (a - high.astype(F32)).astype(BF16)


def dot3(a, b, dims=NN):
    a_high, a_low = split(a)
    b_high, b_low = split(b)
    dot = partial(lax.dot_general, dimension_numbers=dims, preferred_element_type=F32)
    return dot(a_high, b_high) + (dot(a_high, b_low) + dot(a_low, b_high))


def lane_block(i):
    return pl.ds(pl.multiple_of(i * LANES, LANES), LANES)


def row_valid(seg, rows):
    place = lax.broadcasted_iota(jnp.int32, (rows, 1), 0)
    return ((place >= seg[0]) & (place < seg[0] + seg[1])).astype(F32), place


def shifted(x, j, place):
    if j == 0:
        return x
    rows = x.shape[0]
    if j > 0:
        return jnp.where(place >= j, pltpu.roll(x, j, 0), 0.0)
    return jnp.where(place < rows + j, pltpu.roll(x, rows + j, 0), 0.0)


def conv_block(i, xbc, taps, bias, valid, place):
    cols = lane_block(i)
    x = xbc[:, cols] * valid
    total = x * taps[CONV - 1 : CONV, cols]
    for j in range(1, CONV):
        total = total + shifted(x, j, place) * taps[CONV - 1 - j : CONV - j, cols]
    return x, bias[:, cols] + valid * total


def conv_back(i, d_act, x, conv, taps, valid, place, d_xbc, g_taps, g_bias):
    cols = lane_block(i)
    sig = jax.nn.sigmoid(conv)
    d_conv = d_act * (sig * (1.0 + conv * (1.0 - sig)))
    g_bias[:, cols] = jnp.sum(d_conv, axis=0, keepdims=True)
    d_sum = d_conv * valid
    d_x = d_sum * taps[CONV - 1 : CONV, cols]
    g_taps[CONV - 1 : CONV, cols] = jnp.sum(d_sum * x, axis=0, keepdims=True)
    for j in range(1, CONV):
        tap = slice(CONV - 1 - j, CONV - j)
        g_taps[tap, cols] = jnp.sum(d_sum * shifted(x, j, place), axis=0, keepdims=True)
        d_x = d_x + shifted(d_sum, -j, place) * taps[tap, cols]
    d_xbc[:, cols] = (d_x * valid).astype(BF16)


def head_spread(dtype):
    head = lax.broadcasted_iota(jnp.int32, (LANES, INNER), 0)
    col = lax.broadcasted_iota(jnp.int32, (LANES, INNER), 1)
    return (col // HEAD_DIM == head).astype(dtype)


def decays(xbc, heads, cum_col, cum_row, steps_full):
    rows = xbc.shape[0]
    raw = xbc[:, XBC:] + heads[0:1, :]
    steps = jnp.maximum(raw, 0.0) + jnp.log1p(jnp.exp(-jnp.abs(raw)))
    log_decay = -steps * heads[1:2, :]
    r = lax.broadcasted_iota(jnp.int32, (rows, rows), 0)
    c = lax.broadcasted_iota(jnp.int32, (rows, rows), 1)
    cumul = lax.dot_general(
        (r >= c).astype(F32), log_decay, NN, precision=HIGH, preferred_element_type=F32
    )
    cum_row[...] = cumul.T[:HEADS, :]
    for h in range(HEADS):
        cum_col[h] = jnp.broadcast_to(cumul[:, h : h + 1], (rows, LANES))
    steps_full[...] = lax.dot_general(
        steps, head_spread(F32), NN, precision=HIGH, preferred_element_type=F32
    )
    return raw, steps, log_decay


def pair_mask(rows):
    return (lax.broadcasted_iota(jnp.int32, (rows, LANES), 1) < HEAD_DIM).astype(F32)


def wide(column, rows):
    return jnp.concatenate([column] * (rows // LANES), axis=1)


def forward_kernel(
    seg, gate, xbc, taps, bias, heads, skip, gain,
    gated, pre_out, mixed, scale,
    cum_col, cum_row, steps_full, bad, gram,
):
    rows = gate.shape[0]
    valid, place = row_valid(seg, rows)
    decays(xbc, heads, cum_col, cum_row, steps_full)
    r = lax.broadcasted_iota(jnp.int32, (rows, rows), 0)
    c = lax.broadcasted_iota(jnp.int32, (rows, rows), 1)
    inside = (r >= c) & (c >= seg[0]) & (r < seg[0] + seg[1])
    bad[...] = jnp.where(inside, 0.0, -1e30)
    write = jax.nn.silu(conv_block(BLOCKS, xbc, taps, bias, valid, place)[1])
    read = jax.nn.silu(conv_block(BLOCKS + 1, xbc, taps, bias, valid, place)[1])
    gram[...] = dot3(read, write, NT)
    first = pair_mask(rows)

    def pair(i, squares):
        cols = lane_block(i)
        values = jax.nn.silu(conv_block(i, xbc, taps, bias, valid, place)[1])
        source = values * steps_full[:, cols]
        pre = jnp.zeros((rows, LANES), F32)
        for half, keep in enumerate((first, 1.0 - first)):
            h = 2 * i + half
            spread = wide(cum_col[h], rows) - cum_row[pl.ds(h, 1), :] + bad[...]
            pre = pre + dot3(jnp.exp(spread) * gram[...], source * keep)
        gate_in = gate[:, cols]
        m = (pre + skip[:, cols] * values) * jax.nn.silu(gate_in)
        pre_out[:, cols] = pre
        mixed[:, cols] = m
        return squares + m * m

    squares = lax.fori_loop(0, BLOCKS, pair, jnp.zeros((rows, LANES), F32))
    inverse = lax.rsqrt(jnp.sum(squares, axis=1, keepdims=True) / INNER + EPS)
    scale[...] = jnp.broadcast_to(inverse, (rows, LANES))

    def finish(i, carry):
        cols = lane_block(i)
        gated[:, cols] = (mixed[:, cols] * inverse * gain[:, cols]).astype(BF16)
        return carry

    lax.fori_loop(0, BLOCKS, finish, 0)


def backward_kernel(
    seg, gate, xbc, taps, bias, heads, skip, gain, pre_out, mixed, scale, d_gated,
    d_gate, d_xbc, g_taps, g_bias, g_gain, g_heads,
    cum_col, cum_row, steps_full, bad, gram, d_gram, d_cum, d_steps, d_skip,
):
    rows = gate.shape[0]
    valid, place = row_valid(seg, rows)
    raw, steps, log_decay = decays(xbc, heads, cum_col, cum_row, steps_full)
    r = lax.broadcasted_iota(jnp.int32, (rows, rows), 0)
    c = lax.broadcasted_iota(jnp.int32, (rows, rows), 1)
    inside = (c >= r) & (r >= seg[0]) & (c < seg[0] + seg[1])
    bad[...] = jnp.where(inside, 0.0, -1e30)
    write_x, write_conv = conv_block(BLOCKS, xbc, taps, bias, valid, place)
    read_x, read_conv = conv_block(BLOCKS + 1, xbc, taps, bias, valid, place)
    write, read = jax.nn.silu(write_conv), jax.nn.silu(read_conv)
    gram[...] = dot3(write, read, NT)
    d_gram[...] = jnp.zeros_like(d_gram)
    first = pair_mask(rows)
    inverse = scale[...]

    def along(i, total):
        cols = lane_block(i)
        return total + d_gated[:, cols] * gain[:, cols] * mixed[:, cols]

    along_sum = lax.fori_loop(0, BLOCKS, along, jnp.zeros((rows, LANES), F32))
    along_sum = jnp.sum(along_sum, axis=1, keepdims=True) / INNER
    back = inverse * inverse * inverse * along_sum

    def pair(i, carry):
        cols = lane_block(i)
        d_out, m = d_gated[:, cols], mixed[:, cols]
        g_gain[:, cols] = jnp.sum(d_out * m * inverse, axis=0, keepdims=True)
        d_m = inverse * (d_out * gain[:, cols]) - m * back
        gate_in = gate[:, cols]
        sig = jax.nn.sigmoid(gate_in)
        x, conv = conv_block(i, xbc, taps, bias, valid, place)
        values = jax.nn.silu(conv)
        pre = pre_out[:, cols]
        d_u = d_m * (gate_in * sig)
        d_g = d_m * (pre + skip[:, cols] * values) * (sig * (1.0 + gate_in * (1.0 - sig)))
        d_gate[:, cols] = d_g.astype(BF16)
        d_skip[:, cols] = jnp.sum(d_u * values, axis=0, keepdims=True)
        step = steps_full[:, cols]
        source = values * step
        d_source = jnp.zeros((rows, LANES), F32)
        for half, keep in enumerate((first, 1.0 - first)):
            h = 2 * i + half
            spread = cum_row[pl.ds(h, 1), :] - wide(cum_col[h], rows) + bad[...]
            decay = jnp.exp(spread)
            d_head = d_u * keep
            d_source = d_source + dot3(decay * gram[...], d_head)
            d_gram[...] += decay * dot3(source, d_head, NT)
        d_cum[:, cols] = d_u * pre - d_source * source
        d_steps[:, cols] = d_source * values
        d_values = skip[:, cols] * d_u + step * d_source
        conv_back(i, d_values, x, conv, taps, valid, place, d_xbc, g_taps, g_bias)
        return carry

    lax.fori_loop(0, BLOCKS, pair, 0)
    d_back = d_gram[...]
    d_write = dot3(d_back, read)
    d_read = dot3(d_back.T, write)
    conv_back(BLOCKS, d_write, write_x, write_conv, taps, valid, place, d_xbc, g_taps, g_bias)
    conv_back(BLOCKS + 1, d_read, read_x, read_conv, taps, valid, place, d_xbc, g_taps, g_bias)
    spread_t = head_spread(F32)
    sums = partial(
        lax.dot_general, dimension_numbers=NT, precision=HIGH, preferred_element_type=F32
    )
    d_cumul = sums(d_cum[...], spread_t)
    d_log = lax.dot_general(
        (c >= r).astype(F32), d_cumul, NN, precision=HIGH, preferred_element_type=F32
    )
    d_log = d_log * valid
    d_step = sums(d_steps[...], spread_t) - d_log * heads[1:2, :]
    lane = lax.broadcasted_iota(jnp.int32, (rows, LANES), 1)
    d_raw = jnp.where(lane < HEADS, d_step * jax.nn.sigmoid(raw) * valid, 0.0)
    d_xbc[:, XBC:] = d_raw.astype(BF16)
    g_heads[...] = jnp.zeros_like(g_heads)
    g_heads[0:1, :] = jnp.sum(d_raw, axis=0, keepdims=True)
    g_heads[1:2, :] = jnp.sum(d_log * log_decay, axis=0, keepdims=True)
    g_heads[2:3, :] = sums(jnp.broadcast_to(d_skip[...], (8, INNER)), spread_t)[0:1, :]


VMEM_SPEC = pl.BlockSpec(memory_space=pltpu.VMEM)
SMEM_SPEC = pl.BlockSpec(memory_space=pltpu.SMEM)


def scratch(rows):
    return [
        pltpu.VMEM((HEADS, rows, LANES), F32),
        pltpu.VMEM((HEADS, rows), F32),
        pltpu.VMEM((rows, INNER), F32),
        pltpu.VMEM((rows, rows), F32),
        pltpu.VMEM((rows, rows), F32),
    ]


def mixer_forward(seg, gate, xbc, taps, bias, heads, skip, gain):
    rows = gate.shape[0]
    return pl.pallas_call(
        forward_kernel,
        out_shape=(
            jax.ShapeDtypeStruct((rows, INNER), BF16),
            jax.ShapeDtypeStruct((rows, INNER), F32),
            jax.ShapeDtypeStruct((rows, INNER), F32),
            jax.ShapeDtypeStruct((rows, LANES), F32),
        ),
        in_specs=[SMEM_SPEC] + [VMEM_SPEC] * 7,
        out_specs=(VMEM_SPEC,) * 4,
        scratch_shapes=scratch(rows),
        cost_estimate=pl.CostEstimate(
            flops=10_000_000_000, bytes_accessed=10_000_000, transcendentals=4_000_000
        ),
        compiler_params=pltpu.CompilerParams(vmem_limit_bytes=32 * 2**20),
        name="mixer_forward",
    )(seg, gate, xbc, taps, bias, heads, skip, gain)


def mixer_backward(seg, gate, xbc, taps, bias, heads, skip, gain, pre_out, mixed, scale, d_gated):
    rows = gate.shape[0]
    return pl.pallas_call(
        backward_kernel,
        out_shape=(
            jax.ShapeDtypeStruct((rows, INNER), BF16),
            jax.ShapeDtypeStruct((rows, TAIL), BF16),
            jax.ShapeDtypeStruct((CONV, XBC), F32),
            jax.ShapeDtypeStruct((1, XBC), F32),
            jax.ShapeDtypeStruct((1, INNER), F32),
            jax.ShapeDtypeStruct((8, LANES), F32),
        ),
        in_specs=[SMEM_SPEC] + [VMEM_SPEC] * 11,
        out_specs=(VMEM_SPEC,) * 6,
        scratch_shapes=scratch(rows)
        + [
            pltpu.VMEM((rows, rows), F32),
            pltpu.VMEM((rows, INNER), F32),
            pltpu.VMEM((rows, INNER), F32),
            pltpu.VMEM((1, INNER), F32),
        ],
        cost_estimate=pl.CostEstimate(
            flops=20_000_000_000, bytes_accessed=16_000_000, transcendentals=4_000_000
        ),
        compiler_params=pltpu.CompilerParams(vmem_limit_bytes=40 * 2**20),
        name="mixer_backward",
    )(seg, gate, xbc, taps, bias, heads, skip, gain, pre_out, mixed, scale, d_gated)


def swap(x, axis, bit):
    count = lax.axis_size(axis)
    return lax.ppermute(x, axis, [(i, i ^ bit) for i in range(count)])


class Route:
    def __init__(self, count, turned):
        bits = [1 << k for k in range(count.bit_length() - 1)]
        low, high = bits[:2], bits[2:]
        self.spread = [0]
        for bit in high[:2]:
            self.spread = self.spread + [s ^ bit for s in self.spread]
        self.line = high[2:] + (low[::-1] if turned else low)
        order = list(self.spread)
        for bit in self.line:
            order = order + [o ^ bit for o in order]
        self.order = [2 * o for o in order] + [2 * o + 1 for o in order]


def gather(x, route, gates=()):
    parts = [x] + [swap(x, "dp", s) for s in route.spread[1:]]
    held = jnp.concatenate(parts, axis=0)
    for bit in route.line[:-1]:
        held = jnp.concatenate([held, swap(held, "dp", bit)], axis=0)
    near = swap(held, "fsdp", 1)
    if route.line:
        far = swap(held, "dp", route.line[-1])
        return [held, far, near, swap(far, "fsdp", 1)]
    return [held, near]


def scatter(own, other, route):
    total = own + swap(other, "fsdp", 1).astype(F32)
    for bit in route.line[::-1]:
        half = total.shape[0] // 2
        total = total[:half] + swap(total[half:].astype(BF16), "dp", bit).astype(F32)
    size = total.shape[0] // len(route.spread)
    sent = total[size:].astype(BF16)
    result = total[:size]
    for k, s in enumerate(route.spread[1:]):
        result = result + swap(sent[k * size : (k + 1) * size], "dp", s).astype(F32)
    return result


def sum_all(x):
    x = x + swap(x, "fsdp", 1)
    bit = 1
    while bit < lax.axis_size("dp"):
        x = x + swap(x, "dp", bit)
        bit *= 2
    return x


def gather_small(x):
    held = jnp.concatenate([x, swap(x, "fsdp", 1)], axis=0)
    bit = 1
    while bit < lax.axis_size("dp"):
        held = jnp.concatenate([held, swap(held, "dp", bit)], axis=0)
        bit *= 2
    return held


def pick(order, size, own):
    width = len(order) * size
    base = np.concatenate([np.arange(size) + o * size for o in order]).astype(np.int32)
    target = jnp.asarray(base) ^ (own * size)
    return (jnp.arange(width, dtype=jnp.int32)[:, None] == target[None, :]).astype(BF16)


def dot(a, b, dims=NN, kind=F32):
    return lax.dot_general(a, b, dims, preferred_element_type=F32).astype(kind)


def dots(a, pieces):
    start, total = 0, None
    for piece in pieces:
        size = piece.shape[0]
        part = dot(a[:, start : start + size], piece)
        total = part if total is None else total + part
        start += size
    return total


def dots_back(a, pieces):
    return jnp.concatenate([dot(a, piece, NT) for piece in pieces], axis=1)


def shards(
    tokens,
    cotangent,
    seq_offsets,
    seq_lengths,
    norm_gain,
    in_weight,
    conv_weight,
    conv_bias,
    gate_gain,
    out_weight,
    step_bias,
    decay_log,
    skip_scale,
):
    length = tokens.shape[1]
    width = tokens.shape[2]
    groups = lax.axis_size("dp")
    devices = groups * lax.axis_size("fsdp")
    core = lax.axis_index("fsdp")
    own = lax.axis_index("dp") * 2 + core
    size = in_weight.shape[0]
    near = core == 0
    route, turned = Route(groups, False), Route(groups, True)

    conv_size, gate_size = conv_weight.shape[0], gate_gain.shape[0]
    small = jnp.concatenate(
        [norm_gain, conv_weight.T.reshape(-1), conv_bias, gate_gain]
    ).reshape(1, -1)
    small = gather_small(small)
    small_pick = pick(list(range(devices)), 1, own)
    small = dot(small_pick, small)
    gain_full = small[:, :size].reshape(1, width)
    at = size
    taps = small[:, at : at + CONV * conv_size].reshape(devices, CONV, conv_size)
    taps = taps.transpose(1, 0, 2).reshape(CONV, XBC)
    at += CONV * conv_size
    bias = small[:, at : at + conv_size].reshape(1, XBC)
    at += conv_size
    gate_full = small[:, at:].reshape(1, INNER)

    tail = jnp.pad(in_weight[:, INNER:], ((0, 0), (0, TAIL + INNER - in_weight.shape[1])))
    w_gate = gather(in_weight[:, :INNER], route)
    w_tail = gather(tail, turned)
    first_out, second_out, _, _ = lax.optimization_barrier(
        (out_weight[:, : INNER // 2], out_weight[:, INNER // 2 :], w_gate[0], w_tail[0])
    )
    w_out_a = gather(first_out, route)
    w_out_b = gather(second_out, turned)

    def exchange(x):
        kept = lax.dynamic_index_in_dim(x, core, 0, False)
        got = swap(lax.dynamic_index_in_dim(x, 1 - core, 0, False), "fsdp", 1)
        return jnp.concatenate(
            [jnp.where(near, kept, got), jnp.where(near, got, kept)], axis=0
        )

    def give_back(x):
        halves = x.reshape(2, length, width)
        kept = lax.dynamic_index_in_dim(halves, core, 0, False)
        got = swap(lax.dynamic_index_in_dim(halves, 1 - core, 0, False), "fsdp", 1)
        return jnp.stack([jnp.where(near, kept, got), jnp.where(near, got, kept)])

    source_b = exchange(tokens)
    cot_b = exchange(cotangent)
    rows = source_b.shape[0]
    seg = jnp.stack(
        [
            lax.dynamic_index_in_dim(seq_offsets[:, 0, 0], core, 0, False),
            lax.dynamic_index_in_dim(seq_lengths[:, 0, 0], core, 0, False),
        ]
    )
    place = jnp.arange(rows, dtype=jnp.int32)
    valid = ((place >= seg[0]) & (place < seg[0] + seg[1]))[:, None]
    order_a, order_b = pick(route.order, size, own), pick(turned.order, size, own)
    source = source_b.astype(F32)
    inverse = lax.rsqrt(jnp.mean(source * source, axis=1, keepdims=True) + EPS)
    normed_b = (source * inverse * gain_full).astype(BF16)
    masked = jnp.where(valid, cot_b, jnp.zeros((), BF16))
    normed_to_a, normed_to_b = dot(normed_b, order_a, kind=BF16), dot(normed_b, order_b, kind=BF16)
    masked_to_a, masked_to_b = dot(masked, order_a, kind=BF16), dot(masked, order_b, kind=BF16)

    pad = LANES - HEADS
    heads = jnp.stack(
        [jnp.pad(step_bias, (0, pad)), jnp.pad(jnp.exp(decay_log), (0, pad))]
    )
    skip = jnp.repeat(skip_scale, HEAD_DIM).reshape(1, INNER)

    gate = dots(normed_to_a, w_gate)
    xbc = dots(normed_to_b, w_tail)
    gated_b, pre_out, mixed, scale = mixer_forward(
        seg, gate, xbc, taps, bias, heads, skip, gate_full
    )
    half = INNER // 2
    half_rows = width // 2

    def partial_sums(rows_by, columns):
        return (
            dot(rows_by[:, :half_rows], columns, TN),
            dot(rows_by[:, half_rows:], columns, TN, BF16),
        )

    sum_out = jnp.concatenate(
        [
            scatter(*partial_sums(masked_to_a, gated_b[:, :half]), route),
            scatter(*partial_sums(masked_to_b, gated_b[:, half:]), turned),
        ],
        axis=1,
    )
    d_gated = jnp.concatenate([dots(masked_to_a, w_out_a), dots(masked_to_b, w_out_b)], axis=1)
    d_gate, d_xbc, g_taps, g_bias, g_gate, g_heads = mixer_backward(
        seg, gate, xbc, taps, bias, heads, skip, gate_full, pre_out, mixed, scale, d_gated
    )
    sum_gate = scatter(*partial_sums(normed_to_a, d_gate), route)
    sum_tail = scatter(*partial_sums(normed_to_b, d_xbc), turned)
    sum_in = jnp.concatenate([sum_gate, sum_tail[:, : in_weight.shape[1] - INNER]], axis=1)

    def home(x, order):
        high = x.astype(BF16)
        low = (x - high.astype(F32)).astype(BF16)
        return dot(high, order, NT) + dot(low, order, NT)

    branch = home(dots_back(gated_b[:, :half], w_out_a), order_a) + home(
        dots_back(gated_b[:, half:], w_out_b), order_b
    )
    output = (source + jnp.where(valid, branch, 0.0)).astype(BF16)
    d_normed = home(dots_back(d_gate, w_gate), order_a) + home(
        dots_back(d_xbc, w_tail), order_b
    )
    d_scaled = d_normed * gain_full
    inner = jnp.mean(d_scaled * source, axis=1, keepdims=True)
    d_source = inverse * d_scaled - source * (inverse * inverse * inverse * inner)
    g_norm = jnp.sum(d_normed * source * inverse, axis=0, keepdims=True)
    input_grad = cot_b.astype(F32) + d_source

    vector = jnp.concatenate(
        [g_taps.reshape(1, -1), g_bias, g_gate, g_norm, g_heads[:3].reshape(1, -1)], axis=1
    )
    vector = sum_all(vector)[0]
    at = CONV * XBC
    total_taps = lax.dynamic_slice_in_dim(
        vector[:at].reshape(CONV, XBC), own * conv_size, conv_size, 1
    ).T
    total_bias = lax.dynamic_slice_in_dim(vector, at + own * conv_size, conv_size)
    at += XBC
    total_gate = lax.dynamic_slice_in_dim(vector, at + own * gate_size, gate_size)
    at += INNER
    total_norm = lax.dynamic_slice_in_dim(vector, at + own * size, size)
    at += width
    return (
        give_back(output),
        give_back(input_grad),
        total_norm,
        sum_in,
        total_taps,
        total_bias,
        total_gate,
        sum_out,
        vector[at : at + HEADS],
        vector[at + LANES : at + LANES + HEADS],
        vector[at + 2 * LANES : at + 2 * LANES + HEADS],
    )


def solution(mesh):
    both = ("dp", "fsdp")
    rows = P(None, both, None)
    return jax.shard_map(
        shards,
        mesh=mesh,
        in_specs=(
            rows,
            rows,
            P(None, "dp", None),
            P(None, "dp", None),
            P(both),
            P(both, None),
            P(both, None),
            P(both),
            P(both),
            P(both, None),
            P(),
            P(),
            P(),
        ),
        out_specs=(
            rows,
            rows,
            P(both),
            P(both, None),
            P(both, None),
            P(both),
            P(both),
            P(both, None),
            P(),
            P(),
            P(),
        ),
        check_vma=False,
    )
```
